512 devices in a mesh: rep: 2 (over core), row: 16 (over y, x), col: 16 (over z).
Axes of the slice: x: 4, y: 4, z: 16, core: 2. Of those that a mesh axis runs over, the one named last changes fastest.
Arguments:
- residual: bfloat16 [16384, 2048], P(('rep', 'row'), 'col'), may hold values from -6 to 6
- post_gain: float32 [2048], replicated, may hold values from 0.25 to 1.75
- w_gate: bfloat16 [2048, 6144], P('row', 'col'), may hold values from -0.125 to 0.125
- w_up: bfloat16 [2048, 6144], P('row', 'col'), may hold values from -0.125 to 0.125
- w_down: bfloat16 [6144, 2048], P('col', 'row'), may hold values from -0.078125 to 0.078125
- next_gain: float32 [2048], replicated, may hold values from 0.25 to 1.75
- w_qkv: bfloat16 [2048, 4096], P('row', 'col'), may hold values from -0.125 to 0.125
- q_gain: float32 [128], replicated, may hold values from 0.25 to 1.75
- k_gain: float32 [128], replicated, may hold values from 0.25 to 1.75
- source: int32 [16384], P(('rep', 'row')), may hold values from 0 to 16383, as said below
Outputs:
- moved_residual: bfloat16 [16384, 2048], P(('rep', 'row'), 'col')
- moved_qkv: bfloat16 [16384, 4096], P(('rep', 'row'), 'col')
The draws below stay inside these ranges and needn't reach their ends.
Inputs may be any that keep to these rules, and one draw needn't show every extreme that they name: source is a permutation of all rows. Rows are grouped in blocks of 512 (block b holds rows b * 512 to (b + 1) * 512 - 1, blocks of replica 0 first); output block b takes its rows from input block b or from the block of the same row index in the other replica, at most 128 of them from the other replica, and some block takes exactly 128. A block takes as many rows from the other replica as it gives to it.
All inputs are finite; a program needn't handle non-finite values.
Results may differ from the reference program's by a relative error of at most 0.0065.
Values may be sent and summed in bfloat16 or wider, within the bound.
A program may use at most 64 MiB of HBM per device.

```python
import jax
import jax.numpy as jnp
from jax import lax

D = 2048
FF = 6144
HEADS = 16
KV_HEADS = 8
HD = 128
TPD = 512
QKV = 4096
MOVE = 128
TOKENS = 16384
N_ROW = 16


def draw_source(key, part):
    count_key, pick_key, rank_key, slot_key = jax.random.split(key, 4)
    moving_count = jax.random.randint(count_key, (N_ROW,), 0, MOVE + 1)
    forced_pair = jax.random.randint(pick_key, (), 0, N_ROW)
    moving_count = jnp.where(jnp.arange(N_ROW) == forced_pair, MOVE, moving_count).astype(jnp.int32)
    rank_keys = jax.random.split(rank_key, 2 * N_ROW)
    slot_keys = jax.random.split(slot_key, 2 * N_ROW)
    order_rank = jax.vmap(lambda subkey: jax.random.permutation(subkey, TPD))(rank_keys).astype(jnp.int32).reshape(2, N_ROW, TPD)
    slot_table = jax.vmap(lambda subkey: jax.random.permutation(subkey, TPD))(slot_keys).astype(jnp.int32).reshape(2, N_ROW, TPD)
    limit = moving_count[None, :, None]
    going = order_rank < limit
    replica = jnp.broadcast_to(jnp.arange(2, dtype=jnp.int32)[:, None, None], (2, N_ROW, TPD))
    row_index = jnp.broadcast_to(jnp.arange(N_ROW, dtype=jnp.int32)[None, :, None], (2, N_ROW, TPD))
    target = jnp.where(going, 1 - replica, replica)
    place = jnp.where(going, TPD - limit + order_rank, order_rank - limit)
    slot_value = slot_table[target, row_index, place]
    destination = ((target * N_ROW + row_index) * TPD + slot_value).reshape(-1)
    return jnp.zeros((TOKENS,), jnp.int32).at[destination].set(jnp.arange(TOKENS, dtype=jnp.int32))


def block_levels(own_key, extent, pieces, smallest, top_value):
    level = 1.0
    for position, parts in pieces:
        heights = jax.random.uniform(jax.random.fold_in(jax.random.fold_in(own_key, 6), position), (parts,), jnp.float32, smallest / len(pieces), top_value / len(pieces))
        level = level * jnp.repeat(jnp.exp(heights), extent[position] // parts).reshape((-1,) + (1,) * (len(extent) - 1 - position))
    return level


def gaussian(rng, shape, scale, most, pieces=(), kind=jnp.bfloat16):
    values = scale * jax.random.normal(rng, shape, jnp.float32)
    if pieces:
        values = values * block_levels(rng, shape, pieces, -0.22, 0.18)
    return jnp.clip(values, -most, most).astype(kind)


def setup_inputs(seed: int = 0) -> dict:
    keys = jax.random.split(jax.random.key(seed), 11)
    return {
        "residual": gaussian(keys[0], (TOKENS, D), 1.0, 6.0, ((0, 32), (1, 16))),
        "post_gain": jnp.clip(1.0 + 0.15 * jax.random.normal(keys[1], (D,), jnp.float32), 0.25, 1.75),
        "w_gate": gaussian(keys[2], (D, FF), D ** -0.5, 0.125, ((0, 16), (1, 16))),
        "w_up": gaussian(keys[3], (D, FF), D ** -0.5, 0.125, ((0, 16), (1, 16))),
        "w_down": gaussian(keys[4], (FF, D), FF ** -0.5, 0.078125, ((0, 16), (1, 16))),
        "next_gain": jnp.clip(1.0 + 0.15 * jax.random.normal(keys[5], (D,), jnp.float32), 0.25, 1.75),
        "w_qkv": gaussian(keys[6], (D, QKV), D ** -0.5, 0.125, ((0, 16), (1, 16))),
        "q_gain": jnp.clip(1.0 + 0.15 * jax.random.normal(keys[7], (HD,), jnp.float32), 0.25, 1.75),
        "k_gain": jnp.clip(1.0 + 0.15 * jax.random.normal(keys[8], (HD,), jnp.float32), 0.25, 1.75),
        "source": draw_source(jax.random.fold_in(keys[10], 71), 0),
    }


epsilon = 1e-06

def normalize(values, gain):
    scale = jax.lax.rsqrt(lax.optimization_barrier(jnp.mean(values * values, axis=-1, keepdims=True)) + epsilon)
    return values * scale * gain

def reference(residual, post_gain, w_gate, w_up, w_down, next_gain, w_qkv, q_gain, k_gain, source):
    stream = residual.astype(jnp.float32)
    normed = normalize(stream, post_gain).astype(jnp.bfloat16)
    gate_proj = jnp.dot(normed, w_gate, preferred_element_type=jnp.float32)
    up_proj = jnp.dot(normed, w_up, preferred_element_type=jnp.float32)
    hidden = (jax.nn.silu(gate_proj) * up_proj).astype(jnp.bfloat16)
    mlp_out = jnp.dot(hidden, w_down, preferred_element_type=jnp.float32)
    new_residual = (stream + mlp_out).astype(jnp.bfloat16)
    next_normed = normalize(new_residual.astype(jnp.float32), next_gain).astype(jnp.bfloat16)
    projected = jnp.dot(next_normed, w_qkv, preferred_element_type=jnp.float32)
    row_count = projected.shape[0]
    query_part = projected[:, :HEADS * HD].reshape(row_count, HEADS, HD)
    key_part = projected[:, HEADS * HD:(HEADS + KV_HEADS) * HD].reshape(row_count, KV_HEADS, HD)
    value_part = projected[:, (HEADS + KV_HEADS) * HD:]
    query_part = normalize(query_part, q_gain).reshape(row_count, HEADS * HD)
    key_part = normalize(key_part, k_gain).reshape(row_count, KV_HEADS * HD)
    qkv = jnp.concatenate([query_part, key_part, value_part], axis=1).astype(jnp.bfloat16)
    moved_residual = jnp.take(new_residual, source, axis=0)
    moved_qkv = jnp.take(qkv, source, axis=0)
    return (moved_residual, moved_qkv)
```

```python
import functools

import jax
import jax.numpy as jnp
from jax import lax
from jax.experimental import pallas as pl
from jax.experimental.pallas import tpu as pltpu
from jax.sharding import PartitionSpec as P

HEADS = 16
KV_HEADS = 8
HD = 128
NX = 4
CHUNKS = 4
MESH = pl.DeviceIdType.MESH
F32 = jnp.float32
BF16 = jnp.bfloat16

epsilon = 1e-06


def step_kernel(
    n, nrow,
    res_ref, pg_ref, wg_ref, wu_ref, wd_ref, ng_ref, wq_ref, qg_ref, kg_ref, src_ref,
    out_r, out_q,
    x, x2, wgu, wdn, wqk, part, ring, first, hidden, onehot, rv, qv,
    a_send, a_recv, r_send, r_recv, b_send, b_recv,
    w_own, w1_send, w1_recv, w2_send, w2_recv, w3_send, w3_recv, p_send, p_recv,
):
    tok, feat = res_ref.shape
    ff = wg_ref.shape[1]
    qkw = wq_ref.shape[1]
    ny = nrow // NX
    ch = tok // CHUNKS
    tm = tok // 2
    width = n * feat
    me = lax.axis_index("col")
    rep = lax.axis_index("rep")
    row = lax.axis_index("row")
    py, px = row // NX, row % NX

    def ahead(k):
        return lax.rem(me + (k + 2 * n), n)

    right, left = ahead(1), ahead(-1)

    def rcopy(src, dst, ssem, rsem, **device):
        return pltpu.make_async_remote_copy(
            src_ref=src, dst_ref=dst, send_sem=ssem, recv_sem=rsem,
            device_id=device, device_id_type=MESH,
        )

    def x_peer(j):
        return py * NX + lax.rem(px + j, NX)

    def y_peer(j):
        return lax.rem(py + j, ny) * NX + px

    barrier = pltpu.get_barrier_semaphore()
    greeted = [dict(col=right), dict(col=left), dict(rep=1 - rep)]
    greeted += [dict(row=x_peer(j)) for j in range(1, NX)]
    greeted += [dict(row=y_peer(j)) for j in range(1, ny)]
    for device in greeted:
        pl.semaphore_signal(barrier, inc=1, device_id=device, device_id_type=MESH)
    pl.semaphore_wait(barrier, len(greeted))

    def hops(d, k):
        return n // 2 - (1 if (k >= CHUNKS // 2) == (d == 0) else 0)

    chains = [(d, k) for k in range(CHUNKS) for d in range(2)]
    most = n // 2

    def rows_of(k):
        return pl.ds(k * ch, ch)

    def gather_hop(buf, send, recv, d, k, s):
        blk = buf.at[ahead(-s if d == 0 else s), rows_of(k)]
        return rcopy(blk, blk, send.at[d, s, k], recv.at[d, s, k], col=right if d == 0 else left)

    def gather_arrival(buf, send, recv, d, k, s):
        blk = buf.at[ahead(-1 - s if d == 0 else 1 + s), rows_of(k)]
        return rcopy(blk, blk, send.at[d, s, k], recv.at[d, s, k], col=right if d == 0 else left)

    def gather_steps(buf, send, recv, lo, hi):
        def body(s, carry):
            for d, k in chains:
                gather_arrival(buf, send, recv, d, k, s).wait_recv()
                gather_hop(buf, send, recv, d, k, s + 1).start()
            return carry

        lax.fori_loop(lo, hi, body, 0)

    def gather_tail(buf, send, recv):
        for d, k in chains:
            gather_arrival(buf, send, recv, d, k, most - 2).wait_recv()
            if hops(d, k) == most:
                gather_hop(buf, send, recv, d, k, most - 1).start()
        for d, k in chains:
            if hops(d, k) == most:
                gather_arrival(buf, send, recv, d, k, most - 1).wait_recv()

    def drain(make, ):
        def body(s, carry):
            for d, k in chains:
                make(d, k, s).wait_send()
            return carry

        lax.fori_loop(0, most - 1, body, 0)
        for d, k in chains:
            if hops(d, k) == most:
                make(d, k, most - 1).wait_send()

    half_ff, half_q = ff // 2, qkw // 2

    def own_part(c, a):
        if a == 0:
            return wg_ref if c == 0 else wu_ref
        if a == 1:
            return wd_ref.at[pl.ds(c * half_ff, half_ff), :]
        return wq_ref.at[:, pl.ds(c * half_q, half_q)]

    def slot(c, a, y, q):
        lanes = pl.ds(pl.multiple_of(q * feat, feat), feat)
        if a == 0:
            return wgu.at[c, y, lanes, :]
        if a == 1:
            return wdn.at[y, pl.ds(c * half_ff, half_ff), lanes]
        return wqk.at[y, lanes, pl.ds(c * half_q, half_q)]

    def group(c, a, i):
        lanes = pl.ds(pl.multiple_of(i * feat, feat), feat)
        if a == 0:
            return wgu.at[0, i] if c == 0 else wgu.at[1, :, lanes, :]
        if a == 1:
            if c == 0:
                return wdn.at[i, pl.ds(0, half_ff), :]
            return wdn.at[:, pl.ds(half_ff, half_ff), lanes]
        if c == 0:
            return wqk.at[i, :, pl.ds(0, half_q)]
        return wqk.at[:, lanes, pl.ds(half_q, half_q)]

    def w_first(c, a, j):
        peer = x_peer(j) if c == 0 else y_peer(j)
        return rcopy(own_part(c, a), slot(c, a, py, px), w1_send.at[a, j - 1], w1_recv.at[a, j - 1], row=peer)

    def w_first_arrival(c, a, j):
        where = (py, lax.rem(px + NX - j, NX)) if c == 0 else (lax.rem(py + ny - j, ny), px)
        peer = x_peer(j) if c == 0 else y_peer(j)
        return rcopy(own_part(c, a), slot(c, a, *where), w1_send.at[a, j - 1], w1_recv.at[a, j - 1], row=peer)

    def w_local(c, a):
        return pltpu.make_async_copy(own_part(c, a), slot(c, a, py, px), w_own.at[a])

    def w_second(c, a, j):
        blk = group(c, a, py if c == 0 else px)
        peer = y_peer(j) if c == 0 else x_peer(j)
        return rcopy(blk, blk, w2_send.at[a, j - 1], w2_recv.at[a, j - 1], row=peer)

    def w_line(c, j):
        return lax.rem(py + ny - j, ny) if c == 0 else lax.rem(px + NX - j, NX)

    def w_second_arrival(c, a, j):
        blk = group(c, a, w_line(c, j))
        peer = y_peer(j) if c == 0 else x_peer(j)
        return rcopy(blk, blk, w2_send.at[a, j - 1], w2_recv.at[a, j - 1], row=peer)

    def w_relay(c, a, j):
        blk = group(c, a, w_line(c, j))
        return rcopy(blk, blk, w3_send.at[a, j], w3_recv.at[a, j], rep=1 - rep)

    def per_core(run):
        for c in range(2):
            pl.when(rep == c)(functools.partial(run, c))

    def stage_one(arrays):
        def run(c):
            for a in arrays:
                w_local(c, a).start()
                for j in range(1, 4):
                    w_first(c, a, j).start()

        per_core(run)

    def stage_two(arrays):
        def run(c):
            for a in arrays:
                w_local(c, a).wait()
                for j in range(1, 4):
                    w_first_arrival(c, a, j).wait_recv()
                for j in range(1, 4):
                    w_second(c, a, j).start()
                w_relay(c, a, 0).start()

        per_core(run)

    def stage_three(arrays):
        def run(c):
            for a in arrays:
                for j in range(1, 4):
                    w_second_arrival(c, a, j).wait_recv()
                    w_relay(c, a, j).start()

        per_core(run)

    def weights_here(arrays):
        def run(c):
            for a in arrays:
                for j in range(4):
                    w_relay(1 - c, a, j).wait_recv()

        per_core(run)

    def weights_sent(arrays):
        def run(c):
            for a in arrays:
                for j in range(1, 4):
                    w_first(c, a, j).wait_send()
                    w_second(c, a, j).wait_send()
                for j in range(4):
                    w_relay(c, a, j).wait_send()

        per_core(run)

    x[me] = res_ref[...]
    for d, k in chains:
        gather_hop(x, a_send, a_recv, d, k, 0).start()
    stage_one((0, 1))
    gather_steps(x, a_send, a_recv, 0, 1)
    stage_two((0, 1))

    mine = (rep * nrow + row) * tok
    other = ((1 - rep) * nrow + row) * tok
    for k in range(tok // HD):
        line = src_ref[k : k + 1, :]
        own = jnp.logical_and(line >= mine, line < mine + tok)
        place = jnp.where(own, line - mine, line - other + tok)
        down = jnp.transpose(jnp.broadcast_to(place, (HD, HD)))
        for b in range(2 * tok // HD):
            lane = lax.broadcasted_iota(jnp.int32, (HD, HD), 1) + b * HD
            onehot[pl.ds(k * HD, HD), pl.ds(b * HD, HD)] = jnp.where(down == lane, 1.0, 0.0).astype(BF16)

    gather_steps(x, a_send, a_recv, 1, most - 2)
    stage_three((0, 1))
    gather_tail(x, a_send, a_recv)
    weights_here((0, 1))

    def sum_first(d, k):
        to = ahead(hops(d, k) if d == 0 else -hops(d, k))
        return to, rcopy(
            first.at[d, k], ring.at[d, 0, k], r_send.at[d, 0, k], r_recv.at[d, 0, k],
            col=right if d == 0 else left,
        )

    def sum_hop(d, k, s):
        if isinstance(s, int) and s == 0:
            return sum_first(d, k)[1]
        return rcopy(
            ring.at[d, s - 1, k], ring.at[d, s, k], r_send.at[d, s, k], r_recv.at[d, s, k],
            col=right if d == 0 else left,
        )

    def sum_arrival(d, k, s):
        return rcopy(
            ring.at[d, s, k], ring.at[d, s, k], r_send.at[d, s, k], r_recv.at[d, s, k],
            col=right if d == 0 else left,
        )

    def scaled(buf, start, count, gain_ref):
        parts = [buf[b, pl.ds(start, count), :].astype(F32) for b in range(n)]
        total = parts[0] * parts[0]
        for p in parts[1:]:
            total = total + p * p
        scale = lax.rsqrt(jnp.sum(total, axis=-1, keepdims=True) / width + epsilon)
        return jnp.concatenate(
            [(p * scale * gain_ref[:, b * feat : (b + 1) * feat]).astype(BF16) for b, p in enumerate(parts)],
            axis=1,
        )

    for h in range(tok // tm):
        normed = scaled(x, h * tm, tm, pg_ref)
        gate = jnp.dot(normed, wgu[0].reshape(width, ff), preferred_element_type=F32)
        up = jnp.dot(normed, wgu[1].reshape(width, ff), preferred_element_type=F32)
        hidden[...] = (gate / (1.0 + jnp.exp(-gate)) * up).astype(BF16)
        for y in range(ny):
            value = jnp.dot(hidden[...], wdn[y], preferred_element_type=F32)
            for q in range(NX):
                part[y * NX + q, pl.ds(h * tm, tm), :] = value[:, q * feat : (q + 1) * feat]
        for d, k in chains:
            if h * tm <= k * ch < (h + 1) * tm:
                to, copy = sum_first(d, k)
                first[d, k] = part[to, rows_of(k), :].astype(BF16)
                copy.start()
    stage_one((2,))

    def sum_forward(d, k, s):
        sum_arrival(d, k, s - 1).wait_recv()
        to = ahead(hops(d, k) - s if d == 0 else s - hops(d, k))
        ring[d, s - 1, k] = (ring[d, s - 1, k].astype(F32) + part[to, rows_of(k), :]).astype(BF16)
        sum_hop(d, k, s).start()

    def sum_steps(lo, hi):
        def body(s, carry):
            for d, k in chains:
                sum_forward(d, k, s)
            return carry

        lax.fori_loop(lo, hi, body, 0)

    sum_steps(1, 3)
    stage_two((2,))
    sum_steps(3, most - 1)
    for d, k in chains:
        if hops(d, k) == most:
            sum_forward(d, k, most - 1)

    def resid_copy(k):
        return rcopy(
            rv.at[0, rows_of(k)], rv.at[1, rows_of(k)], p_send.at[0, k], p_recv.at[0, k], rep=1 - rep
        )

    def qkv_copy(k):
        return rcopy(
            qv.at[0, rows_of(k)], qv.at[1, rows_of(k)], p_send.at[1, k], p_recv.at[1, k], rep=1 - rep
        )

    for k in range(CHUNKS):
        total = part[me, rows_of(k), :]
        for d in range(2):
            last = hops(d, k) - 1
            sum_arrival(d, k, last).wait_recv()
            total = total + ring[d, last, k].astype(F32)
        fresh = (res_ref[rows_of(k), :].astype(F32) + total).astype(BF16)
        x2[me, rows_of(k), :] = fresh
        rv[0, rows_of(k), :] = fresh
        for d in range(2):
            gather_hop(x2, b_send, b_recv, d, k, 0).start()
        resid_copy(k).start()

    stage_three((2,))
    gather_steps(x2, b_send, b_recv, 0, most - 3)
    for k in range(CHUNKS):
        resid_copy(k).wait_recv()
    out_r[...] = (
        jnp.dot(onehot[:, :tok], rv[0], preferred_element_type=F32)
        + jnp.dot(onehot[:, tok:], rv[1], preferred_element_type=F32)
    ).astype(BF16)
    gather_steps(x2, b_send, b_recv, most - 3, most - 2)
    gather_tail(x2, b_send, b_recv)
    weights_here((2,))

    for h in range(tok // tm):
        normed = scaled(x2, h * tm, tm, ng_ref)
        projected = jnp.dot(normed, wqk[...].reshape(width, qkw), preferred_element_type=F32)
        for i in range(qkw // HD):
            head = me * (qkw // HD) + i
            value = projected[:, i * HD : (i + 1) * HD]
            scale = lax.rsqrt(jnp.mean(value * value, axis=-1, keepdims=True) + epsilon)
            gain = jnp.where(jnp.full((1, HD), head, jnp.int32) < HEADS, qg_ref[...], kg_ref[...])
            normal = jnp.full((tm, HD), head, jnp.int32) < HEADS + KV_HEADS
            qv[0, pl.ds(h * tm, tm), i * HD : (i + 1) * HD] = jnp.where(
                normal, value * scale * gain, value
            ).astype(BF16)
        for k in range(CHUNKS):
            if h * tm <= k * ch < (h + 1) * tm:
                qkv_copy(k).start()

    drain(lambda d, k, s: gather_hop(x, a_send, a_recv, d, k, s))
    drain(lambda d, k, s: rcopy(
        ring.at[d, s, k], ring.at[d, s, k], r_send.at[d, s, k], r_recv.at[d, s, k],
        col=right if d == 0 else left,
    ))
    drain(lambda d, k, s: gather_hop(x2, b_send, b_recv, d, k, s))
    weights_sent((0, 1, 2))
    for k in range(CHUNKS):
        resid_copy(k).wait_send()
        qkv_copy(k).wait_send()
        qkv_copy(k).wait_recv()
    out_q[...] = (
        jnp.dot(onehot[:, :tok], qv[0], preferred_element_type=F32)
        + jnp.dot(onehot[:, tok:], qv[1], preferred_element_type=F32)
    ).astype(BF16)


def per_device(residual, post_gain, w_gate, w_up, w_down, next_gain, w_qkv, q_gain, k_gain, source):
    n = lax.axis_size("col")
    nrow = lax.axis_size("row")
    ny = nrow // NX
    tok, feat = residual.shape
    ff = w_gate.shape[1]
    qkw = w_qkv.shape[1]
    ch = tok // CHUNKS
    most = n // 2
    ring_sems = pltpu.SemaphoreType.DMA((2, most, CHUNKS))
    return pl.pallas_call(
        functools.partial(step_kernel, n, nrow),
        out_shape=(
            jax.ShapeDtypeStruct((tok, feat), BF16),
            jax.ShapeDtypeStruct((tok, qkw), BF16),
        ),
        in_specs=[pl.BlockSpec(memory_space=pltpu.VMEM)] * 10,
        out_specs=(pl.BlockSpec(memory_space=pltpu.VMEM),) * 2,
        scratch_shapes=[
            pltpu.VMEM((n, tok, feat), BF16),
            pltpu.VMEM((n, tok, feat), BF16),
            pltpu.VMEM((2, ny, NX * feat, ff), BF16),
            pltpu.VMEM((ny, ff, NX * feat), BF16),
            pltpu.VMEM((ny, NX * feat, qkw), BF16),
            pltpu.VMEM((n, tok, feat), F32),
            pltpu.VMEM((2, most, CHUNKS, ch, feat), BF16),
            pltpu.VMEM((2, CHUNKS, ch, feat), BF16),
            pltpu.VMEM((tok // 2, ff), BF16),
            pltpu.VMEM((tok, 2 * tok), BF16),
            pltpu.VMEM((2, tok, feat), BF16),
            pltpu.VMEM((2, tok, qkw), BF16),
            ring_sems, ring_sems, ring_sems, ring_sems, ring_sems, ring_sems,
            pltpu.SemaphoreType.DMA((3,)),
            pltpu.SemaphoreType.DMA((3, 3)),
            pltpu.SemaphoreType.DMA((3, 3)),
            pltpu.SemaphoreType.DMA((3, 3)),
            pltpu.SemaphoreType.DMA((3, 3)),
            pltpu.SemaphoreType.DMA((3, 4)),
            pltpu.SemaphoreType.DMA((3, 4)),
            pltpu.SemaphoreType.DMA((2, CHUNKS)),
            pltpu.SemaphoreType.DMA((2, CHUNKS)),
        ],
        compiler_params=pltpu.CompilerParams(
            collective_id=0, has_side_effects=True, vmem_limit_bytes=48 * 1024 * 1024
        ),
        name="block_step",
    )(
        residual, post_gain.reshape(1, -1), w_gate, w_up, w_down, next_gain.reshape(1, -1), w_qkv,
        q_gain.reshape(1, -1), k_gain.reshape(1, -1), source.reshape(-1, HD),
    )


def solution(mesh):
    return jax.shard_map(
        per_device,
        mesh=mesh,
        in_specs=(
            P(("rep", "row"), "col"),
            P(),
            P("row", "col"),
            P("row", "col"),
            P("col", "row"),
            P(),
            P("row", "col"),
            P(),
            P(),
            P(("rep", "row")),
        ),
        out_specs=(P(("rep", "row"), "col"), P(("rep", "row"), "col")),
        check_vma=False,
    )
```

```python
import functools

import jax
import jax.numpy as jnp
from jax import lax
from jax.experimental import pallas as pl
from jax.experimental.pallas import tpu as pltpu
from jax.sharding import PartitionSpec as P

HEADS = 16
KV_HEADS = 8
HD = 128
NX = 4
CHUNKS = 4
MESH = pl.DeviceIdType.MESH
F32 = jnp.float32
BF16 = jnp.bfloat16

epsilon = 1e-06


def step_kernel(
    n, nrow,
    res_hbm, pg_hbm, wg_hbm, wu_hbm, wd_hbm, ng_hbm, wq_hbm, qg_hbm, kg_hbm, src_hbm,
    out_r, out_q,
    pg_ref, ng_ref, qg_ref, kg_ref, src_ref,
    x, x2, wgu, wdn, wqk, gated, squares, proj, part, ring, first, onehot, rv, qv,
    a_send, a_recv, r_send, r_recv, b_send, b_recv,
    small, w_own, w1_send, w1_recv, w2_send, w2_recv, w3_send, w3_recv, p_send, p_recv,
):
    tok, feat = res_hbm.shape
    ff = wg_hbm.shape[1]
    qkw = wq_hbm.shape[1]
    ny = nrow // NX
    ch = tok // CHUNKS
    tm = tok // 2
    width = n * feat
    me = lax.axis_index("col")
    rep = lax.axis_index("rep")
    row = lax.axis_index("row")
    py, px = row // NX, row % NX

    def ahead(k):
        return lax.rem(me + (k + 2 * n), n)

    right, left = ahead(1), ahead(-1)

    def rcopy(src, dst, ssem, rsem, **device):
        return pltpu.make_async_remote_copy(
            src_ref=src, dst_ref=dst, send_sem=ssem, recv_sem=rsem,
            device_id=device, device_id_type=MESH,
        )

    def x_peer(j):
        return py * NX + lax.rem(px + j, NX)

    def y_peer(j):
        return lax.rem(py + j, ny) * NX + px

    loads = [
        pltpu.make_async_copy(src, dst, small.at[i])
        for i, (src, dst) in enumerate((
            (res_hbm, x.at[me]), (src_hbm, src_ref), (pg_hbm, pg_ref),
            (ng_hbm, ng_ref), (qg_hbm, qg_ref), (kg_hbm, kg_ref),
        ))
    ]
    for load in loads:
        load.start()

    barrier = pltpu.get_barrier_semaphore()
    greeted = [dict(col=right), dict(col=left), dict(rep=1 - rep)]
    greeted += [dict(row=x_peer(j)) for j in range(1, NX)]
    greeted += [dict(row=y_peer(j)) for j in range(1, ny)]
    for device in greeted:
        pl.semaphore_signal(barrier, inc=1, device_id=device, device_id_type=MESH)
    pl.semaphore_wait(barrier, len(greeted))

    def hops(d, k):
        return n // 2 - (1 if (k >= CHUNKS // 2) == (d == 0) else 0)

    chains = [(d, k) for k in range(CHUNKS) for d in range(2)]
    most = n // 2
    halves = tok // tm

    def rows_of(k):
        return pl.ds(k * ch, ch)

    def in_half(h):
        return [(d, k) for d, k in chains if h * tm <= k * ch < (h + 1) * tm]

    def gather_hop(buf, send, recv, d, k, s):
        blk = buf.at[ahead(-s if d == 0 else s), rows_of(k)]
        return rcopy(blk, blk, send.at[d, s, k], recv.at[d, s, k], col=right if d == 0 else left)

    def gather_arrival(buf, send, recv, d, k, s):
        blk = buf.at[ahead(-1 - s if d == 0 else 1 + s), rows_of(k)]
        return rcopy(blk, blk, send.at[d, s, k], recv.at[d, s, k], col=right if d == 0 else left)

    def first_hop(d, k):
        return rcopy(
            res_hbm.at[rows_of(k)], x.at[me, rows_of(k)], a_send.at[d, 0, k], a_recv.at[d, 0, k],
            col=right if d == 0 else left,
        )

    def gather_step(buf, send, recv, s, group):
        for d, k in group:
            gather_arrival(buf, send, recv, d, k, s).wait_recv()
            if not isinstance(s, int) or s + 1 < hops(d, k):
                gather_hop(buf, send, recv, d, k, s + 1).start()

    def gather_steps(buf, send, recv, lo, hi, extra=None):
        def body(s, carry):
            gather_step(buf, send, recv, s, chains)
            if extra is not None:
                extra(s)
            return carry

        lax.fori_loop(lo, hi, body, 0)

    def last_arrivals(buf, send, recv, group):
        for d, k in group:
            if hops(d, k) == most:
                gather_arrival(buf, send, recv, d, k, most - 1).wait_recv()

    def sent(make, s):
        for d, k in chains:
            if not isinstance(s, int) or s < hops(d, k):
                make(d, k, s).wait_send()

    half_ff, half_q = ff // 2, qkw // 2

    def own_part(c, a):
        if a == 0:
            return wg_hbm if c == 0 else wu_hbm
        if a == 1:
            return wd_hbm.at[pl.ds(c * half_ff, half_ff), :]
        return wq_hbm.at[:, pl.ds(c * half_q, half_q)]

    def slot(c, a, y, q):
        if a == 0:
            return wgu.at[c, y, q]
        if a == 1:
            return wdn.at[y, pl.ds(c * half_ff, half_ff), pl.ds(pl.multiple_of(q * feat, feat), feat)]
        return wqk.at[y, q, :, pl.ds(c * half_q, half_q)]

    def group(c, a, i):
        if a == 0:
            return wgu.at[0, i] if c == 0 else wgu.at[1, :, i]
        if a == 1:
            if c == 0:
                return wdn.at[i, pl.ds(0, half_ff), :]
            return wdn.at[:, pl.ds(half_ff, half_ff), pl.ds(pl.multiple_of(i * feat, feat), feat)]
        if c == 0:
            return wqk.at[i, :, :, pl.ds(0, half_q)]
        return wqk.at[:, i, :, pl.ds(half_q, half_q)]

    def w_first(c, a, j):
        peer = x_peer(j) if c == 0 else y_peer(j)
        return rcopy(own_part(c, a), slot(c, a, py, px), w1_send.at[a, j - 1], w1_recv.at[a, j - 1], row=peer)

    def w_first_arrival(c, a, j):
        where = (py, lax.rem(px + NX - j, NX)) if c == 0 else (lax.rem(py + ny - j, ny), px)
        peer = x_peer(j) if c == 0 else y_peer(j)
        return rcopy(own_part(c, a), slot(c, a, *where), w1_send.at[a, j - 1], w1_recv.at[a, j - 1], row=peer)

    def w_local(c, a):
        return pltpu.make_async_copy(own_part(c, a), slot(c, a, py, px), w_own.at[a])

    def w_second(c, a, j):
        blk = group(c, a, py if c == 0 else px)
        peer = y_peer(j) if c == 0 else x_peer(j)
        return rcopy(blk, blk, w2_send.at[a, j - 1], w2_recv.at[a, j - 1], row=peer)

    def w_line(c, j):
        return lax.rem(py + ny - j, ny) if c == 0 else lax.rem(px + NX - j, NX)

    def w_second_arrival(c, a, j):
        blk = group(c, a, w_line(c, j))
        peer = y_peer(j) if c == 0 else x_peer(j)
        return rcopy(blk, blk, w2_send.at[a, j - 1], w2_recv.at[a, j - 1], row=peer)

    def w_relay(c, a, j):
        blk = group(c, a, w_line(c, j))
        return rcopy(blk, blk, w3_send.at[a, j], w3_recv.at[a, j], rep=1 - rep)

    def per_core(run):
        for c in range(2):
            pl.when(rep == c)(functools.partial(run, c))

    def stage_one(arrays):
        def run(c):
            for a in arrays:
                for j in range(1, 4):
                    w_first(c, a, j).start()
                w_local(c, a).start()

        per_core(run)

    def stage_two(arrays):
        def run(c):
            for a in arrays:
                w_local(c, a).wait()
                for j in range(1, 4):
                    w_first_arrival(c, a, j).wait_recv()
                for j in range(1, 4):
                    w_second(c, a, j).start()
                w_relay(c, a, 0).start()

        per_core(run)

    def stage_three(arrays):
        def run(c):
            for a in arrays:
                for j in range(1, 4):
                    w_second_arrival(c, a, j).wait_recv()
                    w_relay(c, a, j).start()

        per_core(run)

    def weights_here(arrays):
        def run(c):
            for a in arrays:
                for j in range(4):
                    w_relay(1 - c, a, j).wait_recv()

        per_core(run)

    def weights_sent(arrays):
        def run(c):
            for a in arrays:
                for j in range(1, 4):
                    w_first(c, a, j).wait_send()
                    w_second(c, a, j).wait_send()
                for j in range(4):
                    w_relay(c, a, j).wait_send()

        per_core(run)

    def pair(s):
        return [me, ahead(most)] if s is None else [ahead(-1 - s), ahead(1 + s)]

    def taken(buf, gain_ref, blocks, rows):
        values = [buf[b, rows, :].astype(F32) for b in blocks]
        square = values[0] * values[0]
        for v in values[1:]:
            square = square + v * v
        lhs = jnp.concatenate([(v * gain_ref[pl.ds(b, 1), :]).astype(BF16) for v, b in zip(values, blocks)], axis=1)
        return square, lhs

    def row_scale(square):
        return lax.rsqrt(jnp.sum(square, axis=-1, keepdims=True) / width + epsilon)

    def gate_up(h, steps, fresh):
        rows = pl.ds(h * tm, tm)
        blocks = [b for s in steps for b in pair(s)]
        square, lhs = taken(x, pg_ref, blocks, rows)
        both = []
        for c in range(2):
            rhs = jnp.concatenate([wgu[c, b // NX, lax.rem(b, NX)] for b in blocks], axis=0)
            both.append(jnp.dot(lhs, rhs, preferred_element_type=F32))
        if not fresh:
            square = square + squares[rows, :]
            both = [v + gated[c, rows, :] for c, v in enumerate(both)]
        return square, both

    def gate_up_add(h, steps, fresh):
        rows = pl.ds(h * tm, tm)
        square, both = gate_up(h, steps, fresh)
        squares[rows, :] = square
        for c in range(2):
            gated[c, rows, :] = both[c]

    stage_one((0,))
    for d, k in chains:
        first_hop(d, k).start()
    stage_one((1,))
    for load in loads:
        load.wait()
    gather_step(x, a_send, a_recv, 0, chains)
    stage_two((0,))
    gather_step(x, a_send, a_recv, 1, chains)
    stage_two((1,))

    mine = (rep * nrow + row) * tok
    other = ((1 - rep) * nrow + row) * tok

    def select_rows(k):
        line = src_ref[pl.ds(k, 1), :]
        own = jnp.logical_and(line >= mine, line < mine + tok)
        place = jnp.where(own, line - mine, line - other + tok)
        down = jnp.transpose(jnp.broadcast_to(place, (HD, HD)))
        for b in range(2 * tok // HD):
            lane = lax.broadcasted_iota(jnp.int32, (HD, HD), 1) + b * HD
            onehot[pl.ds(pl.multiple_of(k * HD, HD), HD), pl.ds(b * HD, HD)] = jnp.where(
                down == lane, 1.0, 0.0
            ).astype(BF16)

    gather_steps(x, a_send, a_recv, 2, most - 3)
    stage_three((0,))
    gather_step(x, a_send, a_recv, most - 3, chains)
    weights_here((0,))
    for h in range(halves):
        gate_up_add(h, (0, 1, 2), True)
    for h in range(halves):
        gather_step(x, a_send, a_recv, most - 2, in_half(h))
    stage_three((1,))
    for h in range(halves):
        gate_up_add(h, (3, 4, 5, 6), False)

    def sum_first(d, k):
        to = ahead(hops(d, k) if d == 0 else -hops(d, k))
        return to, rcopy(
            first.at[d, k], ring.at[d, 0, k], r_send.at[d, 0, k], r_recv.at[d, 0, k],
            col=right if d == 0 else left,
        )

    def sum_hop(d, k, s):
        return rcopy(
            ring.at[d, s - 1, k], ring.at[d, s, k], r_send.at[d, s, k], r_recv.at[d, s, k],
            col=right if d == 0 else left,
        )

    def sum_arrival(d, k, s):
        return rcopy(
            ring.at[d, s, k], ring.at[d, s, k], r_send.at[d, s, k], r_recv.at[d, s, k],
            col=right if d == 0 else left,
        )

    for h in range(halves):
        last_arrivals(x, a_send, a_recv, in_half(h))
        square, (gate, up) = gate_up(h, (None,), False)
        scale = row_scale(square)
        gate = gate * scale
        up = up * scale
        hidden = (gate / (1.0 + jnp.exp(-gate)) * up).astype(BF16)
        if h == 0:
            weights_here((1,))
        for y in range(ny):
            value = jnp.dot(hidden, wdn[y], preferred_element_type=F32)
            for q in range(NX):
                part[y * NX + q, pl.ds(h * tm, tm), :] = value[:, q * feat : (q + 1) * feat]
        for d, k in in_half(h):
            to, copy = sum_first(d, k)
            first[d, k] = part[to, rows_of(k), :].astype(BF16)
            copy.start()
    stage_one((2,))

    def sum_forward(d, k, s):
        sum_arrival(d, k, s - 1).wait_recv()
        to = ahead(hops(d, k) - s if d == 0 else s - hops(d, k))
        ring[d, s - 1, k] = (ring[d, s - 1, k].astype(F32) + part[to, rows_of(k), :]).astype(BF16)
        sum_hop(d, k, s).start()

    def a_hop(d, k, s):
        return gather_hop(x, a_send, a_recv, d, k, s)

    def sum_steps(lo, hi):
        def body(s, carry):
            for d, k in chains:
                sum_forward(d, k, s)
            sent(a_hop, s - 1)
            return carry

        lax.fori_loop(lo, hi, body, 0)

    sum_steps(1, 3)
    stage_two((2,))
    sum_steps(3, most - 1)
    for k in range(tok // HD):
        select_rows(k)
    for d, k in chains:
        if hops(d, k) == most:
            sum_forward(d, k, most - 1)
    sent(a_hop, most - 2)
    sent(a_hop, most - 1)

    def resid_copy(k):
        return rcopy(
            rv.at[0, rows_of(k)], rv.at[1, rows_of(k)], p_send.at[0, k], p_recv.at[0, k], rep=1 - rep
        )

    def qkv_copy(k):
        return rcopy(
            qv.at[0, rows_of(k)], qv.at[1, rows_of(k)], p_send.at[1, k], p_recv.at[1, k], rep=1 - rep
        )

    for k in range(CHUNKS):
        total = part[me, rows_of(k), :]
        for d in range(2):
            last = hops(d, k) - 1
            sum_arrival(d, k, last).wait_recv()
            total = total + ring[d, last, k].astype(F32)
        fresh = (x[me, rows_of(k), :].astype(F32) + total).astype(BF16)
        x2[me, rows_of(k), :] = fresh
        rv[0, rows_of(k), :] = fresh
        for d in range(2):
            gather_hop(x2, b_send, b_recv, d, k, 0).start()
        resid_copy(k).start()

    stage_three((2,))

    def qkv_part(rows, s, fresh):
        blocks = pair(s)
        square, lhs = taken(x2, ng_ref, blocks, rows)
        rhs = jnp.concatenate([wqk[b // NX, lax.rem(b, NX)] for b in blocks], axis=0)
        value = jnp.dot(lhs, rhs, preferred_element_type=F32)
        if not fresh:
            square = square + squares[rows, :]
            value = value + proj[rows, :]
        return square, value

    def qkv_add(s, fresh):
        for h in range(halves):
            rows = pl.ds(h * tm, tm)
            square, value = qkv_part(rows, s, fresh)
            squares[rows, :] = square
            proj[rows, :] = value

    def b_hop(d, k, s):
        return gather_hop(x2, b_send, b_recv, d, k, s)

    gather_step(x2, b_send, b_recv, 0, chains)
    weights_here((2,))
    qkv_add(0, True)
    sent(sum_arrival, 0)
    weights_sent((0, 1, 2))

    def later(s):
        qkv_add(s, False)
        sent(sum_arrival, s)
        sent(b_hop, s - 1)

    gather_steps(x2, b_send, b_recv, 1, most - 3, later)
    for k in range(CHUNKS):
        resid_copy(k).wait_recv()
    out_r[...] = (
        jnp.dot(onehot[:, :tok], rv[0], preferred_element_type=F32)
        + jnp.dot(onehot[:, tok:], rv[1], preferred_element_type=F32)
    ).astype(BF16)
    gather_steps(x2, b_send, b_recv, most - 3, most - 2, later)
    gather_step(x2, b_send, b_recv, most - 2, chains)
    qkv_add(most - 2, False)
    sent(sum_arrival, most - 2)
    sent(sum_arrival, most - 1)
    sent(b_hop, most - 3)

    for h in range(halves):
        last_arrivals(x2, b_send, b_recv, in_half(h))
        rows = pl.ds(h * tm, tm)
        square, projected = qkv_part(rows, None, False)
        projected = projected * row_scale(square)
        for i in range(qkw // HD):
            head = me * (qkw // HD) + i
            value = projected[:, i * HD : (i + 1) * HD]
            scale = lax.rsqrt(jnp.mean(value * value, axis=-1, keepdims=True) + epsilon)
            gain = jnp.where(jnp.full((1, HD), head, jnp.int32) < HEADS, qg_ref[...], kg_ref[...])
            normal = jnp.full((tm, HD), head, jnp.int32) < HEADS + KV_HEADS
            qv[0, rows, i * HD : (i + 1) * HD] = jnp.where(normal, value * scale * gain, value).astype(BF16)
        for k in range(CHUNKS):
            if h * tm <= k * ch < (h + 1) * tm:
                qkv_copy(k).start()

    own_rows = jnp.dot(onehot[:, :tok], qv[0], preferred_element_type=F32)
    sent(b_hop, most - 2)
    sent(b_hop, most - 1)
    for k in range(CHUNKS):
        resid_copy(k).wait_send()
        qkv_copy(k).wait_send()
        qkv_copy(k).wait_recv()
    out_q[...] = (own_rows + jnp.dot(onehot[:, tok:], qv[1], preferred_element_type=F32)).astype(BF16)


def per_device(residual, post_gain, w_gate, w_up, w_down, next_gain, w_qkv, q_gain, k_gain, source):
    n = lax.axis_size("col")
    nrow = lax.axis_size("row")
    ny = nrow // NX
    tok, feat = residual.shape
    ff = w_gate.shape[1]
    qkw = w_qkv.shape[1]
    ch = tok // CHUNKS
    most = n // 2
    ring_sems = pltpu.SemaphoreType.DMA((2, most, CHUNKS))
    return pl.pallas_call(
        functools.partial(step_kernel, n, nrow),
        out_shape=(
            jax.ShapeDtypeStruct((tok, feat), BF16),
            jax.ShapeDtypeStruct((tok, qkw), BF16),
        ),
        in_specs=[pl.BlockSpec(memory_space=pl.ANY)] * 10,
        out_specs=(pl.BlockSpec(memory_space=pltpu.VMEM),) * 2,
        scratch_shapes=[
            pltpu.VMEM((n, feat), F32),
            pltpu.VMEM((n, feat), F32),
            pltpu.VMEM((1, HD), F32),
            pltpu.VMEM((1, HD), F32),
            pltpu.VMEM((tok // HD, HD), jnp.int32),
            pltpu.VMEM((n, tok, feat), BF16),
            pltpu.VMEM((n, tok, feat), BF16),
            pltpu.VMEM((2, ny, NX, feat, ff), BF16),
            pltpu.VMEM((ny, ff, NX * feat), BF16),
            pltpu.VMEM((ny, NX, feat, qkw), BF16),
            pltpu.VMEM((2, tok, ff), F32),
            pltpu.VMEM((tok, feat), F32),
            pltpu.VMEM((tok, qkw), F32),
            pltpu.VMEM((n, tok, feat), F32),
            pltpu.VMEM((2, most, CHUNKS, ch, feat), BF16),
            pltpu.VMEM((2, CHUNKS, ch, feat), BF16),
            pltpu.VMEM((tok, 2 * tok), BF16),
            pltpu.VMEM((2, tok, feat), BF16),
            pltpu.VMEM((2, tok, qkw), BF16),
            ring_sems, ring_sems, ring_sems, ring_sems, ring_sems, ring_sems,
            pltpu.SemaphoreType.DMA((6,)),
            pltpu.SemaphoreType.DMA((3,)),
            pltpu.SemaphoreType.DMA((3, 3)),
            pltpu.SemaphoreType.DMA((3, 3)),
            pltpu.SemaphoreType.DMA((3, 3)),
            pltpu.SemaphoreType.DMA((3, 3)),
            pltpu.SemaphoreType.DMA((3, 4)),
            pltpu.SemaphoreType.DMA((3, 4)),
            pltpu.SemaphoreType.DMA((2, CHUNKS)),
            pltpu.SemaphoreType.DMA((2, CHUNKS)),
        ],
        compiler_params=pltpu.CompilerParams(
            collective_id=0, has_side_effects=True, vmem_limit_bytes=60 * 1024 * 1024
        ),
        name="block_step",
    )(
        residual, post_gain.reshape(n, feat), w_gate, w_up, w_down, next_gain.reshape(n, feat), w_qkv,
        q_gain.reshape(1, -1), k_gain.reshape(1, -1), source.reshape(-1, HD),
    )


def solution(mesh):
    return jax.shard_map(
        per_device,
        mesh=mesh,
        in_specs=(
            P(("rep", "row"), "col"),
            P(),
            P("row", "col"),
            P("row", "col"),
            P("col", "row"),
            P(),
            P("row", "col"),
            P(),
            P(),
            P(("rep", "row")),
        ),
        out_specs=(P(("rep", "row"), "col"), P(("rep", "row"), "col")),
        check_vma=False,
    )
```

```python
import functools

import jax
import jax.numpy as jnp
from jax import lax
from jax.experimental import pallas as pl
from jax.experimental.pallas import tpu as pltpu
from jax.sharding import PartitionSpec as P

HEADS = 16
KV_HEADS = 8
HD = 128
NX = 4
CHUNKS = 4
MESH = pl.DeviceIdType.MESH
F32 = jnp.float32
BF16 = jnp.bfloat16

epsilon = 1e-06


def step_kernel(
    n, nrow,
    res_hbm, pg_hbm, wg_hbm, wu_hbm, wd_hbm, ng_hbm, wq_hbm, qg_hbm, kg_hbm, src_hbm,
    out_r, out_q,
    pg_ref, ng_ref, qg_ref, kg_ref, src_ref,
    x, x2, wgu, wdn, wqk, hidden, gated, squares, proj, part, ring, first, onehot, rv, qv,
    a_send, a_recv, r_send, r_recv, b_send, b_recv,
    small, w_own, w1_send, w1_recv, w2_send, w2_recv, w3_send, w3_recv, p_send, p_recv,
):
    tok, feat = res_hbm.shape
    ff = wg_hbm.shape[1]
    qkw = wq_hbm.shape[1]
    ny = nrow // NX
    ch = tok // CHUNKS
    tm = tok // 2
    width = n * feat
    me = lax.axis_index("col")
    rep = lax.axis_index("rep")
    row = lax.axis_index("row")
    py, px = row // NX, row % NX

    def ahead(k):
        return lax.rem(me + (k + 2 * n), n)

    def along(d, k):
        return ahead(k if d == 0 else -k)

    onward = [along(0, 1), along(1, 1)]

    def rcopy(src, dst, ssem, rsem, **device):
        return pltpu.make_async_remote_copy(
            src_ref=src, dst_ref=dst, send_sem=ssem, recv_sem=rsem,
            device_id=device, device_id_type=MESH,
        )

    def x_peer(j):
        return py * NX + lax.rem(px + j, NX)

    def y_peer(j):
        return lax.rem(py + j, ny) * NX + px

    loads = [
        pltpu.make_async_copy(src, dst, small.at[i])
        for i, (src, dst) in enumerate((
            (res_hbm, x.at[me]), (src_hbm, src_ref), (pg_hbm, pg_ref),
            (ng_hbm, ng_ref), (qg_hbm, qg_ref), (kg_hbm, kg_ref),
        ))
    ]
    for load in loads:
        load.start()

    barrier = pltpu.get_barrier_semaphore()
    greeted = [dict(col=onward[0]), dict(col=onward[1]), dict(rep=1 - rep)]
    greeted += [dict(row=x_peer(j)) for j in range(1, NX)]
    greeted += [dict(row=y_peer(j)) for j in range(1, ny)]
    for device in greeted:
        pl.semaphore_signal(barrier, inc=1, device_id=device, device_id_type=MESH)
    pl.semaphore_wait(barrier, len(greeted))

    def hops(d, k):
        return n // 2 - (1 if (k >= CHUNKS // 2) == (d == 0) else 0)

    chains = [(d, k) for k in range(CHUNKS) for d in range(2)]
    most = n // 2
    halves = tok // tm

    def rows_of(k):
        return pl.ds(k * ch, ch)

    def in_half(h):
        return [(d, k) for d, k in chains if h * tm <= k * ch < (h + 1) * tm]

    def gather_hop(buf, send, recv, d, k, s):
        blk = buf.at[along(d, -s), rows_of(k)]
        return rcopy(blk, blk, send.at[d, s, k], recv.at[d, s, k], col=onward[d])

    def gather_arrival(buf, send, recv, d, k, s):
        blk = buf.at[along(d, -1 - s), rows_of(k)]
        return rcopy(blk, blk, send.at[d, s, k], recv.at[d, s, k], col=onward[d])

    def gather_step(buf, send, recv, s, group):
        for d, k in group:
            gather_arrival(buf, send, recv, d, k, s).wait_recv()
            if s + 1 < hops(d, k):
                gather_hop(buf, send, recv, d, k, s + 1).start()

    def gather_steps(buf, send, recv, lo, hi, extra=None):
        for s in range(lo, hi):
            gather_step(buf, send, recv, s, chains)
            if extra is not None:
                extra(s)

    def last_arrivals(buf, send, recv, group):
        for d, k in group:
            if hops(d, k) == most:
                gather_arrival(buf, send, recv, d, k, most - 1).wait_recv()

    def sent(make, s):
        for d, k in chains:
            if s < hops(d, k):
                make(d, k, s).wait_send()

    half_ff, half_q = ff // 2, qkw // 2

    def own_part(c, a):
        if a == 0:
            return wg_hbm if c == 0 else wu_hbm
        if a == 1:
            return wd_hbm.at[pl.ds(c * half_ff, half_ff), :]
        return wq_hbm.at[:, pl.ds(c * half_q, half_q)]

    def slot(c, a, y, q):
        if a == 0:
            return wgu.at[c, y, q]
        if a == 1:
            return wdn.at[y, pl.ds(c * half_ff, half_ff), pl.ds(pl.multiple_of(q * feat, feat), feat)]
        return wqk.at[y, q, :, pl.ds(c * half_q, half_q)]

    def group(c, a, i):
        if a == 0:
            return wgu.at[0, i] if c == 0 else wgu.at[1, :, i]
        if a == 1:
            if c == 0:
                return wdn.at[i, pl.ds(0, half_ff), :]
            return wdn.at[:, pl.ds(half_ff, half_ff), pl.ds(pl.multiple_of(i * feat, feat), feat)]
        if c == 0:
            return wqk.at[i, :, :, pl.ds(0, half_q)]
        return wqk.at[:, i, :, pl.ds(half_q, half_q)]

    def w_first(c, a, j):
        peer = x_peer(j) if c == 0 else y_peer(j)
        return rcopy(own_part(c, a), slot(c, a, py, px), w1_send.at[a, j - 1], w1_recv.at[a, j - 1], row=peer)

    def w_first_arrival(c, a, j):
        where = (py, lax.rem(px + NX - j, NX)) if c == 0 else (lax.rem(py + ny - j, ny), px)
        peer = x_peer(j) if c == 0 else y_peer(j)
        return rcopy(own_part(c, a), slot(c, a, *where), w1_send.at[a, j - 1], w1_recv.at[a, j - 1], row=peer)

    def w_local(c, a):
        return pltpu.make_async_copy(own_part(c, a), slot(c, a, py, px), w_own.at[a])

    def w_second(c, a, j):
        blk = group(c, a, py if c == 0 else px)
        peer = y_peer(j) if c == 0 else x_peer(j)
        return rcopy(blk, blk, w2_send.at[a, j - 1], w2_recv.at[a, j - 1], row=peer)

    def w_line(c, j):
        return lax.rem(py + ny - j, ny) if c == 0 else lax.rem(px + NX - j, NX)

    def w_second_arrival(c, a, j):
        blk = group(c, a, w_line(c, j))
        peer = y_peer(j) if c == 0 else x_peer(j)
        return rcopy(blk, blk, w2_send.at[a, j - 1], w2_recv.at[a, j - 1], row=peer)

    def w_relay(c, a, j):
        blk = group(c, a, w_line(c, j))
        return rcopy(blk, blk, w3_send.at[a, j], w3_recv.at[a, j], rep=1 - rep)

    def per_core(run):
        for c in range(2):
            pl.when(rep == c)(functools.partial(run, c))

    def stage_one(arrays):
        def run(c):
            for a in arrays:
                for j in range(1, 4):
                    w_first(c, a, j).start()
                w_local(c, a).start()

        per_core(run)

    def stage_two(arrays):
        def run(c):
            for a in arrays:
                w_local(c, a).wait()
                for j in range(1, 4):
                    w_first_arrival(c, a, j).wait_recv()
                for j in range(1, 4):
                    w_second(c, a, j).start()
                w_relay(c, a, 0).start()

        per_core(run)

    def stage_three(arrays):
        def run(c):
            for a in arrays:
                for j in range(1, 4):
                    w_second_arrival(c, a, j).wait_recv()
                    w_relay(c, a, j).start()

        per_core(run)

    def weights_here(arrays):
        def run(c):
            for a in arrays:
                for j in range(4):
                    w_relay(1 - c, a, j).wait_recv()

        per_core(run)

    def weights_sent(arrays):
        def run(c):
            for a in arrays:
                for j in range(1, 4):
                    w_first(c, a, j).wait_send()
                    w_second(c, a, j).wait_send()
                for j in range(4):
                    w_relay(c, a, j).wait_send()

        per_core(run)

    def pair(s):
        return [me, ahead(most)] if s is None else [ahead(-1 - s), ahead(1 + s)]

    def taken(buf, gain_ref, blocks, rows):
        values = [buf[b, rows, :].astype(F32) for b in blocks]
        square = values[0] * values[0]
        for v in values[1:]:
            square = square + v * v
        lhs = jnp.concatenate([(v * gain_ref[pl.ds(b, 1), :]).astype(BF16) for v, b in zip(values, blocks)], axis=1)
        return square, lhs

    def row_scale(square):
        return lax.rsqrt(jnp.sum(square, axis=-1, keepdims=True) / width + epsilon)

    def gate_up(h, steps, fresh):
        rows = pl.ds(h * tm, tm)
        blocks = [b for s in steps for b in pair(s)]
        square, lhs = taken(x, pg_ref, blocks, rows)
        both = []
        for c in range(2):
            rhs = jnp.concatenate([wgu[c, b // NX, lax.rem(b, NX)] for b in blocks], axis=0)
            both.append(jnp.dot(lhs, rhs, preferred_element_type=F32))
        if not fresh:
            square = square + squares[rows, :]
            both = [v + gated[c, rows, :] for c, v in enumerate(both)]
        return square, both

    def gate_up_add(h, steps, fresh):
        rows = pl.ds(h * tm, tm)
        square, both = gate_up(h, steps, fresh)
        squares[rows, :] = square
        for c in range(2):
            gated[c, rows, :] = both[c]

    loads[0].wait()
    for d, k in chains:
        gather_hop(x, a_send, a_recv, d, k, 0).start()
    stage_one((0, 1))
    for load in loads[1:]:
        load.wait()
    gather_step(x, a_send, a_recv, 0, chains)
    stage_two((0,))
    gather_step(x, a_send, a_recv, 1, chains)
    stage_two((1,))

    mine = (rep * nrow + row) * tok
    other = ((1 - rep) * nrow + row) * tok

    def select_rows(k):
        line = src_ref[pl.ds(k, 1), :]
        own = jnp.logical_and(line >= mine, line < mine + tok)
        place = jnp.where(own, line - mine, line - other + tok)
        down = jnp.transpose(jnp.broadcast_to(place, (HD, HD)))
        for b in range(2 * tok // HD):
            lane = lax.broadcasted_iota(jnp.int32, (HD, HD), 1) + b * HD
            onehot[pl.ds(pl.multiple_of(k * HD, HD), HD), pl.ds(b * HD, HD)] = jnp.where(
                down == lane, 1.0, 0.0
            ).astype(BF16)

    gather_steps(x, a_send, a_recv, 2, most - 3)
    stage_three((0,))
    gather_step(x, a_send, a_recv, most - 3, chains)
    weights_here((0,))
    for h in range(halves):
        gate_up_add(h, (0, 1, 2), True)
    for h in range(halves):
        gather_step(x, a_send, a_recv, most - 2, in_half(h))
    stage_three((1,))
    for h in range(halves):
        gate_up_add(h, (3, 4, 5, 6), False)

    def sum_first(d, k):
        to = along(d, hops(d, k))
        return to, rcopy(
            first.at[d, k], ring.at[d, 0, k], r_send.at[d, 0, k], r_recv.at[d, 0, k],
            col=onward[d],
        )

    def sum_hop(d, k, s):
        return rcopy(
            ring.at[d, s - 1, k], ring.at[d, s, k], r_send.at[d, s, k], r_recv.at[d, s, k],
            col=onward[d],
        )

    def sum_arrival(d, k, s):
        return rcopy(
            ring.at[d, s, k], ring.at[d, s, k], r_send.at[d, s, k], r_recv.at[d, s, k],
            col=onward[d],
        )

    far_line = lax.rem(me + most - 1, n) // NX

    def down_lines(h, lines):
        for i in lines:
            y = lax.rem(far_line + i, ny)
            value = jnp.dot(hidden[pl.ds(h * tm, tm), :], wdn[y], preferred_element_type=F32)
            for q in range(NX):
                part[y * NX + q, pl.ds(h * tm, tm), :] = value[:, q * feat : (q + 1) * feat]

    for h in range(halves):
        last_arrivals(x, a_send, a_recv, in_half(h))
        square, (gate, up) = gate_up(h, (None,), False)
        scale = row_scale(square)
        gate = gate * scale
        up = up * scale
        hidden[pl.ds(h * tm, tm), :] = (gate / (1.0 + jnp.exp(-gate)) * up).astype(BF16)
        if h == 0:
            weights_here((1,))
        down_lines(h, (0, 1))
        for d, k in in_half(h):
            to, copy = sum_first(d, k)
            first[d, k] = part[to, rows_of(k), :].astype(BF16)
            copy.start()
    for h in range(halves):
        down_lines(h, range(2, ny))
    stage_one((2,))

    def sum_forward(d, k, s):
        sum_arrival(d, k, s - 1).wait_recv()
        to = along(d, hops(d, k) - s)
        ring[d, s - 1, k] = (ring[d, s - 1, k].astype(F32) + part[to, rows_of(k), :]).astype(BF16)
        sum_hop(d, k, s).start()

    def a_hop(d, k, s):
        return gather_hop(x, a_send, a_recv, d, k, s)

    def sum_steps(lo, hi):
        for s in range(lo, hi):
            for d, k in chains:
                sum_forward(d, k, s)
            sent(a_hop, s - 1)

    sum_steps(1, 3)
    stage_two((2,))
    sum_steps(3, most - 1)
    for d, k in chains:
        if hops(d, k) == most:
            sum_forward(d, k, most - 1)
    sent(a_hop, most - 2)
    sent(a_hop, most - 1)

    def resid_copy(k):
        return rcopy(
            rv.at[0, rows_of(k)], rv.at[1, rows_of(k)], p_send.at[0, k], p_recv.at[0, k], rep=1 - rep
        )

    def qkv_copy(k):
        return rcopy(
            qv.at[0, rows_of(k)], qv.at[1, rows_of(k)], p_send.at[1, k], p_recv.at[1, k], rep=1 - rep
        )

    for k in range(CHUNKS):
        total = part[me, rows_of(k), :]
        for d in range(2):
            last = hops(d, k) - 1
            sum_arrival(d, k, last).wait_recv()
            total = total + ring[d, last, k].astype(F32)
        fresh = (x[me, rows_of(k), :].astype(F32) + total).astype(BF16)
        x2[me, rows_of(k), :] = fresh
        rv[0, rows_of(k), :] = fresh
        for d in range(2):
            gather_hop(x2, b_send, b_recv, d, k, 0).start()
        resid_copy(k).start()

    stage_three((2,))

    def qkv_part(rows, blocks, fresh):
        square, lhs = taken(x2, ng_ref, blocks, rows)
        rhs = jnp.concatenate([wqk[b // NX, lax.rem(b, NX)] for b in blocks], axis=0)
        value = jnp.dot(lhs, rhs, preferred_element_type=F32)
        if not fresh:
            square = square + squares[rows, :]
            value = value + proj[rows, :]
        return square, value

    def qkv_add(s, fresh):
        for h in range(halves):
            rows = pl.ds(h * tm, tm)
            square, value = qkv_part(rows, pair(s), fresh)
            squares[rows, :] = square
            proj[rows, :] = value

    quarters = tok // HD

    def b_hop(d, k, s):
        return gather_hop(x2, b_send, b_recv, d, k, s)

    gather_step(x2, b_send, b_recv, 0, chains)
    weights_here((2,))
    qkv_add(0, True)
    sent(sum_arrival, 0)
    weights_sent((0, 1, 2))

    def later(s):
        qkv_add(s, False)
        sent(sum_arrival, s)
        sent(b_hop, s - 1)

    def later_select(s):
        later(s)
        for k in range(quarters * (s - 1) // (most - 4), quarters * s // (most - 4)):
            select_rows(k)

    gather_steps(x2, b_send, b_recv, 1, most - 3, later_select)
    for k in range(CHUNKS):
        resid_copy(k).wait_recv()
    out_r[...] = (
        jnp.dot(onehot[:, :tok], rv[0], preferred_element_type=F32)
        + jnp.dot(onehot[:, tok:], rv[1], preferred_element_type=F32)
    ).astype(BF16)
    gather_steps(x2, b_send, b_recv, most - 3, most - 2, later)
    gather_step(x2, b_send, b_recv, most - 2, chains)
    qkv_add(most - 2, False)
    sent(sum_arrival, most - 2)
    sent(sum_arrival, most - 1)
    sent(b_hop, most - 3)

    for k in range(CHUNKS):
        last_arrivals(x2, b_send, b_recv, [(d, i) for d, i in chains if i == k])
        rows = rows_of(k)
        square, projected = qkv_part(rows, pair(None), False)
        projected = projected * row_scale(square)
        for i in range(qkw // HD):
            head = me * (qkw // HD) + i
            value = projected[:, i * HD : (i + 1) * HD]
            scale = lax.rsqrt(jnp.mean(value * value, axis=-1, keepdims=True) + epsilon)
            gain = jnp.where(jnp.full((1, HD), head, jnp.int32) < HEADS, qg_ref[...], kg_ref[...])
            normal = jnp.full((ch, HD), head, jnp.int32) < HEADS + KV_HEADS
            qv[0, rows, i * HD : (i + 1) * HD] = jnp.where(normal, value * scale * gain, value).astype(BF16)
        qkv_copy(k).start()

    own_rows = jnp.dot(onehot[:, :tok], qv[0], preferred_element_type=F32)
    sent(b_hop, most - 2)
    sent(b_hop, most - 1)
    for k in range(CHUNKS):
        resid_copy(k).wait_send()
        qkv_copy(k).wait_send()
        qkv_copy(k).wait_recv()
    out_q[...] = (own_rows + jnp.dot(onehot[:, tok:], qv[1], preferred_element_type=F32)).astype(BF16)


def per_device(residual, post_gain, w_gate, w_up, w_down, next_gain, w_qkv, q_gain, k_gain, source):
    n = lax.axis_size("col")
    nrow = lax.axis_size("row")
    ny = nrow // NX
    tok, feat = residual.shape
    ff = w_gate.shape[1]
    qkw = w_qkv.shape[1]
    ch = tok // CHUNKS
    most = n // 2
    ring_sems = pltpu.SemaphoreType.DMA((2, most, CHUNKS))
    return pl.pallas_call(
        functools.partial(step_kernel, n, nrow),
        out_shape=(
            jax.ShapeDtypeStruct((tok, feat), BF16),
            jax.ShapeDtypeStruct((tok, qkw), BF16),
        ),
        in_specs=[pl.BlockSpec(memory_space=pl.ANY)] * 10,
        out_specs=(pl.BlockSpec(memory_space=pltpu.VMEM),) * 2,
        scratch_shapes=[
            pltpu.VMEM((n, feat), F32),
            pltpu.VMEM((n, feat), F32),
            pltpu.VMEM((1, HD), F32),
            pltpu.VMEM((1, HD), F32),
            pltpu.VMEM((tok // HD, HD), jnp.int32),
            pltpu.VMEM((n, tok, feat), BF16),
            pltpu.VMEM((n, tok, feat), BF16),
            pltpu.VMEM((2, ny, NX, feat, ff), BF16),
            pltpu.VMEM((ny, ff, NX * feat), BF16),
            pltpu.VMEM((ny, NX, feat, qkw), BF16),
            pltpu.VMEM((tok, ff), BF16),
            pltpu.VMEM((2, tok, ff), F32),
            pltpu.VMEM((tok, feat), F32),
            pltpu.VMEM((tok, qkw), F32),
            pltpu.VMEM((n, tok, feat), F32),
            pltpu.VMEM((2, most, CHUNKS, ch, feat), BF16),
            pltpu.VMEM((2, CHUNKS, ch, feat), BF16),
            pltpu.VMEM((tok, 2 * tok), BF16),
            pltpu.VMEM((2, tok, feat), BF16),
            pltpu.VMEM((2, tok, qkw), BF16),
            ring_sems, ring_sems, ring_sems, ring_sems, ring_sems, ring_sems,
            pltpu.SemaphoreType.DMA((6,)),
            pltpu.SemaphoreType.DMA((3,)),
            pltpu.SemaphoreType.DMA((3, 3)),
            pltpu.SemaphoreType.DMA((3, 3)),
            pltpu.SemaphoreType.DMA((3, 3)),
            pltpu.SemaphoreType.DMA((3, 3)),
            pltpu.SemaphoreType.DMA((3, 4)),
            pltpu.SemaphoreType.DMA((3, 4)),
            pltpu.SemaphoreType.DMA((2, CHUNKS)),
            pltpu.SemaphoreType.DMA((2, CHUNKS)),
        ],
        compiler_params=pltpu.CompilerParams(
            collective_id=0, has_side_effects=True, vmem_limit_bytes=60 * 1024 * 1024
        ),
        name="block_step",
    )(
        residual, post_gain.reshape(n, feat), w_gate, w_up, w_down, next_gain.reshape(n, feat), w_qkv,
        q_gain.reshape(1, -1), k_gain.reshape(1, -1), source.reshape(-1, HD),
    )


def solution(mesh):
    return jax.shard_map(
        per_device,
        mesh=mesh,
        in_specs=(
            P(("rep", "row"), "col"),
            P(),
            P("row", "col"),
            P("row", "col"),
            P("col", "row"),
            P(),
            P("row", "col"),
            P(),
            P(),
            P(("rep", "row")),
        ),
        out_specs=(P(("rep", "row"), "col"), P(("rep", "row"), "col")),
        check_vma=False,
    )
```

```python
import functools

import jax
import jax.numpy as jnp
from jax import lax
from jax.experimental import pallas as pl
from jax.experimental.pallas import tpu as pltpu
from jax.sharding import PartitionSpec as P

HEADS = 16
KV_HEADS = 8
HD = 128
NX = 4
CHUNKS = 4
MESH = pl.DeviceIdType.MESH
F32 = jnp.float32
BF16 = jnp.bfloat16

epsilon = 1e-06


def step_kernel(
    n, nrow,
    res_hbm, pg_hbm, wg_hbm, wu_hbm, wd_hbm, ng_hbm, wq_hbm, qg_hbm, kg_hbm, src_hbm,
    out_r, out_q,
    pg_ref, ng_ref, qg_ref, kg_ref, src_ref,
    x, x2, wgu, wdn, wqk, hidden, gated, squares, proj, part, ring, first, onehot, rv, qv,
    a_send, a_recv, r_send, r_recv, b_send, b_recv,
    small, w_own, w1_send, w1_recv, w2_send, w2_recv, w3_send, w3_recv, p_send, p_recv,
):
    tok, feat = res_hbm.shape
    ff = wg_hbm.shape[1]
    qkw = wq_hbm.shape[1]
    ny = nrow // NX
    ch = tok // CHUNKS
    tm = tok // 2
    width = n * feat
    me = lax.axis_index("col")
    rep = lax.axis_index("rep")
    row = lax.axis_index("row")
    py, px = row // NX, row % NX

    def ahead(k):
        return lax.rem(me + (k + 2 * n), n)

    def along(d, k):
        return ahead(k if d == 0 else -k)

    onward = [along(0, 1), along(1, 1)]
    beyond = [along(0, 2), along(1, 2)]

    def rcopy(src, dst, ssem, rsem, **device):
        return pltpu.make_async_remote_copy(
            src_ref=src, dst_ref=dst, send_sem=ssem, recv_sem=rsem,
            device_id=device, device_id_type=MESH,
        )

    def x_peer(j):
        return py * NX + lax.rem(px + j, NX)

    def y_peer(j):
        return lax.rem(py + j, ny) * NX + px

    loads = [
        pltpu.make_async_copy(src, dst, small.at[i])
        for i, (src, dst) in enumerate((
            (res_hbm, x.at[me]), (src_hbm, src_ref), (pg_hbm, pg_ref),
            (ng_hbm, ng_ref), (qg_hbm, qg_ref), (kg_hbm, kg_ref),
        ))
    ]
    for load in loads:
        load.start()

    barrier = pltpu.get_barrier_semaphore()
    greeted = [dict(col=c) for c in onward + beyond] + [dict(rep=1 - rep)]
    greeted += [dict(row=x_peer(j)) for j in range(1, NX)]
    greeted += [dict(row=y_peer(j)) for j in range(1, ny)]
    for device in greeted:
        pl.semaphore_signal(barrier, inc=1, device_id=device, device_id_type=MESH)
    pl.semaphore_wait(barrier, len(greeted))

    def hops(d, k):
        return n // 2 - (1 if (k >= CHUNKS // 2) == (d == 0) else 0)

    chains = [(d, k) for k in range(CHUNKS) for d in range(2)]
    most = n // 2
    halves = tok // tm

    def rows_of(k):
        return pl.ds(k * ch, ch)

    def in_half(h):
        return [(d, k) for d, k in chains if h * tm <= k * ch < (h + 1) * tm]

    def gather_hop(buf, send, recv, d, k, s):
        blk = buf.at[along(d, -s), rows_of(k)]
        return rcopy(blk, blk, send.at[d, s, k], recv.at[d, s, k], col=onward[d])

    def gather_arrival(buf, send, recv, d, k, s):
        blk = buf.at[along(d, -1 - s), rows_of(k)]
        return rcopy(blk, blk, send.at[d, s, k], recv.at[d, s, k], col=onward[d])

    def gather_step(buf, send, recv, s, group):
        for d, k in group:
            gather_arrival(buf, send, recv, d, k, s).wait_recv()
            if s + 1 < most - 1:
                gather_hop(buf, send, recv, d, k, s + 1).start()
            if s == most - 3 and hops(d, k) == most:
                blk = buf.at[along(d, -1 - s), rows_of(k)]
                rcopy(blk, blk, send.at[d, most - 1, k], recv.at[d, most - 1, k], col=beyond[d]).start()

    def gather_steps(buf, send, recv, lo, hi, extra=None):
        for s in range(lo, hi):
            gather_step(buf, send, recv, s, chains)
            if extra is not None:
                extra(s)

    def last_arrivals(buf, send, recv, group):
        for d, k in group:
            if hops(d, k) == most:
                gather_arrival(buf, send, recv, d, k, most - 1).wait_recv()

    def sent(make, s):
        for d, k in chains:
            if s < hops(d, k):
                make(d, k, s).wait_send()

    half_ff, half_q = ff // 2, qkw // 2

    def own_part(c, a):
        if a == 0:
            return wg_hbm if c == 0 else wu_hbm
        if a == 1:
            return wd_hbm.at[pl.ds(c * half_ff, half_ff), :]
        return wq_hbm.at[:, pl.ds(c * half_q, half_q)]

    def slot(c, a, y, q):
        if a == 0:
            return wgu.at[c, y, q]
        if a == 1:
            return wdn.at[y, pl.ds(c * half_ff, half_ff), pl.ds(pl.multiple_of(q * feat, feat), feat)]
        return wqk.at[y, q, :, pl.ds(c * half_q, half_q)]

    def group(c, a, i):
        if a == 0:
            return wgu.at[0, i] if c == 0 else wgu.at[1, :, i]
        if a == 1:
            if c == 0:
                return wdn.at[i, pl.ds(0, half_ff), :]
            return wdn.at[:, pl.ds(half_ff, half_ff), pl.ds(pl.multiple_of(i * feat, feat), feat)]
        if c == 0:
            return wqk.at[i, :, :, pl.ds(0, half_q)]
        return wqk.at[:, i, :, pl.ds(half_q, half_q)]

    def w_first(c, a, j):
        peer = x_peer(j) if c == 0 else y_peer(j)
        return rcopy(own_part(c, a), slot(c, a, py, px), w1_send.at[a, j - 1], w1_recv.at[a, j - 1], row=peer)

    def w_first_arrival(c, a, j):
        where = (py, lax.rem(px + NX - j, NX)) if c == 0 else (lax.rem(py + ny - j, ny), px)
        peer = x_peer(j) if c == 0 else y_peer(j)
        return rcopy(own_part(c, a), slot(c, a, *where), w1_send.at[a, j - 1], w1_recv.at[a, j - 1], row=peer)

    def w_local(c, a):
        return pltpu.make_async_copy(own_part(c, a), slot(c, a, py, px), w_own.at[a])

    def w_second(c, a, j):
        blk = group(c, a, py if c == 0 else px)
        peer = y_peer(j) if c == 0 else x_peer(j)
        return rcopy(blk, blk, w2_send.at[a, j - 1], w2_recv.at[a, j - 1], row=peer)

    def w_line(c, j):
        return lax.rem(py + ny - j, ny) if c == 0 else lax.rem(px + NX - j, NX)

    def w_second_arrival(c, a, j):
        blk = group(c, a, w_line(c, j))
        peer = y_peer(j) if c == 0 else x_peer(j)
        return rcopy(blk, blk, w2_send.at[a, j - 1], w2_recv.at[a, j - 1], row=peer)

    def w_relay(c, a, j):
        blk = group(c, a, w_line(c, j))
        return rcopy(blk, blk, w3_send.at[a, j], w3_recv.at[a, j], rep=1 - rep)

    def per_core(run):
        for c in range(2):
            pl.when(rep == c)(functools.partial(run, c))

    def stage_one(arrays):
        def run(c):
            for a in arrays:
                for j in range(1, 4):
                    w_first(c, a, j).start()
                w_local(c, a).start()

        per_core(run)

    def stage_two(arrays):
        def run(c):
            for a in arrays:
                w_local(c, a).wait()
                for j in range(1, 4):
                    w_first_arrival(c, a, j).wait_recv()
                for j in range(1, 4):
                    w_second(c, a, j).start()
                w_relay(c, a, 0).start()

        per_core(run)

    def stage_three(arrays):
        def run(c):
            for a in arrays:
                for j in range(1, 4):
                    w_second_arrival(c, a, j).wait_recv()
                    w_relay(c, a, j).start()

        per_core(run)

    def weights_here(arrays):
        def run(c):
            for a in arrays:
                for j in range(4):
                    w_relay(1 - c, a, j).wait_recv()

        per_core(run)

    def weights_sent(arrays):
        def run(c):
            for a in arrays:
                for j in range(1, 4):
                    w_first(c, a, j).wait_send()
                    w_second(c, a, j).wait_send()
                for j in range(4):
                    w_relay(c, a, j).wait_send()

        per_core(run)

    def pair(s):
        return [me, ahead(most)] if s is None else [ahead(-1 - s), ahead(1 + s)]

    def taken(buf, gain_ref, blocks, rows):
        values = [buf[b, rows, :].astype(F32) for b in blocks]
        square = values[0] * values[0]
        for v in values[1:]:
            square = square + v * v
        lhs = jnp.concatenate([(v * gain_ref[pl.ds(b, 1), :]).astype(BF16) for v, b in zip(values, blocks)], axis=1)
        return square, lhs

    def row_scale(square):
        return lax.rsqrt(jnp.sum(square, axis=-1, keepdims=True) / width + epsilon)

    def gate_up(h, steps, fresh):
        rows = pl.ds(h * tm, tm)
        blocks = [b for s in steps for b in pair(s)]
        square, lhs = taken(x, pg_ref, blocks, rows)
        both = []
        for c in range(2):
            rhs = jnp.concatenate([wgu[c, b // NX, lax.rem(b, NX)] for b in blocks], axis=0)
            both.append(jnp.dot(lhs, rhs, preferred_element_type=F32))
        if not fresh:
            square = square + squares[rows, :]
            both = [v + gated[c, rows, :] for c, v in enumerate(both)]
        return square, both

    def gate_up_add(h, steps, fresh):
        rows = pl.ds(h * tm, tm)
        square, both = gate_up(h, steps, fresh)
        squares[rows, :] = square
        for c in range(2):
            gated[c, rows, :] = both[c]

    loads[0].wait()
    for d, k in chains:
        gather_hop(x, a_send, a_recv, d, k, 0).start()
    stage_one((0, 1))
    for load in loads[1:]:
        load.wait()
    gather_step(x, a_send, a_recv, 0, chains)
    stage_two((0,))
    gather_step(x, a_send, a_recv, 1, chains)
    stage_two((1,))

    mine = (rep * nrow + row) * tok
    other = ((1 - rep) * nrow + row) * tok

    def select_rows(k):
        line = src_ref[pl.ds(k, 1), :]
        own = jnp.logical_and(line >= mine, line < mine + tok)
        place = jnp.where(own, line - mine, line - other + tok)
        down = jnp.transpose(jnp.broadcast_to(place, (HD, HD)))
        for b in range(2 * tok // HD):
            lane = lax.broadcasted_iota(jnp.int32, (HD, HD), 1) + b * HD
            onehot[pl.ds(pl.multiple_of(k * HD, HD), HD), pl.ds(b * HD, HD)] = jnp.where(
                down == lane, 1.0, 0.0
            ).astype(BF16)

    gather_steps(x, a_send, a_recv, 2, most - 3)
    stage_three((0,))
    gather_step(x, a_send, a_recv, most - 3, chains)
    weights_here((0,))
    for h in range(halves):
        gate_up_add(h, (0, 1, 2), True)
    for h in range(halves):
        gather_step(x, a_send, a_recv, most - 2, in_half(h))
    stage_three((1,))
    for h in range(halves):
        gate_up_add(h, (3, 4, 5, 6), False)

    def sum_first(d, k):
        to = along(d, hops(d, k))
        return to, rcopy(
            first.at[d, k], ring.at[d, 0, k], r_send.at[d, 0, k], r_recv.at[d, 0, k],
            col=onward[d],
        )

    def sum_hop(d, k, s):
        return rcopy(
            ring.at[d, s - 1, k], ring.at[d, s, k], r_send.at[d, s, k], r_recv.at[d, s, k],
            col=onward[d],
        )

    def sum_arrival(d, k, s):
        return rcopy(
            ring.at[d, s, k], ring.at[d, s, k], r_send.at[d, s, k], r_recv.at[d, s, k],
            col=onward[d],
        )

    far_line = lax.rem(me + most - 1, n) // NX

    def down_lines(h, lines):
        for i in lines:
            y = lax.rem(far_line + i, ny)
            value = jnp.dot(hidden[pl.ds(h * tm, tm), :], wdn[y], preferred_element_type=F32)
            for q in range(NX):
                part[y * NX + q, pl.ds(h * tm, tm), :] = value[:, q * feat : (q + 1) * feat]

    for h in range(halves):
        last_arrivals(x, a_send, a_recv, in_half(h))
        square, (gate, up) = gate_up(h, (None,), False)
        scale = row_scale(square)
        gate = gate * scale
        up = up * scale
        hidden[pl.ds(h * tm, tm), :] = (gate / (1.0 + jnp.exp(-gate)) * up).astype(BF16)
        if h == 0:
            weights_here((1,))
        down_lines(h, (0, 1))
        for d, k in in_half(h):
            to, copy = sum_first(d, k)
            first[d, k] = part[to, rows_of(k), :].astype(BF16)
            copy.start()
    for h in range(halves):
        down_lines(h, range(2, ny))
    stage_one((2,))

    def sum_forward(d, k, s):
        sum_arrival(d, k, s - 1).wait_recv()
        to = along(d, hops(d, k) - s)
        ring[d, s - 1, k] = (ring[d, s - 1, k].astype(F32) + part[to, rows_of(k), :]).astype(BF16)
        sum_hop(d, k, s).start()

    def a_hop(d, k, s):
        return gather_hop(x, a_send, a_recv, d, k, s)

    def sum_steps(lo, hi):
        for s in range(lo, hi):
            for d, k in chains:
                sum_forward(d, k, s)
            sent(a_hop, s - 1)

    sum_steps(1, 3)
    stage_two((2,))
    sum_steps(3, most - 1)
    for d, k in chains:
        if hops(d, k) == most:
            sum_forward(d, k, most - 1)
    sent(a_hop, most - 2)
    sent(a_hop, most - 1)

    def resid_copy(k):
        return rcopy(
            rv.at[0, rows_of(k)], rv.at[1, rows_of(k)], p_send.at[0, k], p_recv.at[0, k], rep=1 - rep
        )

    def qkv_copy(k):
        return rcopy(
            qv.at[0, rows_of(k)], qv.at[1, rows_of(k)], p_send.at[1, k], p_recv.at[1, k], rep=1 - rep
        )

    for k in range(CHUNKS):
        total = part[me, rows_of(k), :]
        for d in range(2):
            last = hops(d, k) - 1
            sum_arrival(d, k, last).wait_recv()
            total = total + ring[d, last, k].astype(F32)
        fresh = (x[me, rows_of(k), :].astype(F32) + total).astype(BF16)
        x2[me, rows_of(k), :] = fresh
        rv[0, rows_of(k), :] = fresh
        for d in range(2):
            gather_hop(x2, b_send, b_recv, d, k, 0).start()
        resid_copy(k).start()

    stage_three((2,))

    def qkv_part(rows, blocks, fresh):
        square, lhs = taken(x2, ng_ref, blocks, rows)
        rhs = jnp.concatenate([wqk[b // NX, lax.rem(b, NX)] for b in blocks], axis=0)
        value = jnp.dot(lhs, rhs, preferred_element_type=F32)
        if not fresh:
            square = square + squares[rows, :]
            value = value + proj[rows, :]
        return square, value

    def qkv_add(s, fresh):
        for h in range(halves):
            rows = pl.ds(h * tm, tm)
            square, value = qkv_part(rows, pair(s), fresh)
            squares[rows, :] = square
            proj[rows, :] = value

    quarters = tok // HD

    def b_hop(d, k, s):
        return gather_hop(x2, b_send, b_recv, d, k, s)

    gather_step(x2, b_send, b_recv, 0, chains)
    weights_here((2,))
    qkv_add(0, True)
    sent(sum_arrival, 0)
    weights_sent((0, 1, 2))

    def later(s):
        qkv_add(s, False)
        sent(sum_arrival, s)
        sent(b_hop, s - 1)

    def later_select(s):
        later(s)
        for k in range(quarters * (s - 1) // (most - 4), quarters * s // (most - 4)):
            select_rows(k)

    gather_steps(x2, b_send, b_recv, 1, most - 3, later_select)
    for k in range(CHUNKS):
        resid_copy(k).wait_recv()
    out_r[...] = (
        jnp.dot(onehot[:, :tok], rv[0], preferred_element_type=F32)
        + jnp.dot(onehot[:, tok:], rv[1], preferred_element_type=F32)
    ).astype(BF16)
    gather_steps(x2, b_send, b_recv, most - 3, most - 2, later)
    gather_step(x2, b_send, b_recv, most - 2, chains)
    qkv_add(most - 2, False)
    sent(sum_arrival, most - 2)
    sent(sum_arrival, most - 1)
    sent(b_hop, most - 3)

    for k in range(CHUNKS):
        last_arrivals(x2, b_send, b_recv, [(d, i) for d, i in chains if i == k])
        rows = rows_of(k)
        square, projected = qkv_part(rows, pair(None), False)
        projected = projected * row_scale(square)
        for i in range(qkw // HD):
            head = me * (qkw // HD) + i
            value = projected[:, i * HD : (i + 1) * HD]
            scale = lax.rsqrt(jnp.mean(value * value, axis=-1, keepdims=True) + epsilon)
            gain = jnp.where(jnp.full((1, HD), head, jnp.int32) < HEADS, qg_ref[...], kg_ref[...])
            normal = jnp.full((ch, HD), head, jnp.int32) < HEADS + KV_HEADS
            qv[0, rows, i * HD : (i + 1) * HD] = jnp.where(normal, value * scale * gain, value).astype(BF16)
        qkv_copy(k).start()

    own_rows = jnp.dot(onehot[:, :tok], qv[0], preferred_element_type=F32)
    sent(b_hop, most - 2)
    sent(b_hop, most - 1)
    for k in range(CHUNKS):
        resid_copy(k).wait_send()
        qkv_copy(k).wait_send()
        qkv_copy(k).wait_recv()
    out_q[...] = (own_rows + jnp.dot(onehot[:, tok:], qv[1], preferred_element_type=F32)).astype(BF16)


def per_device(residual, post_gain, w_gate, w_up, w_down, next_gain, w_qkv, q_gain, k_gain, source):
    n = lax.axis_size("col")
    nrow = lax.axis_size("row")
    ny = nrow // NX
    tok, feat = residual.shape
    ff = w_gate.shape[1]
    qkw = w_qkv.shape[1]
    ch = tok // CHUNKS
    most = n // 2
    ring_sems = pltpu.SemaphoreType.DMA((2, most, CHUNKS))
    return pl.pallas_call(
        functools.partial(step_kernel, n, nrow),
        out_shape=(
            jax.ShapeDtypeStruct((tok, feat), BF16),
            jax.ShapeDtypeStruct((tok, qkw), BF16),
        ),
        in_specs=[pl.BlockSpec(memory_space=pl.ANY)] * 10,
        out_specs=(pl.BlockSpec(memory_space=pltpu.VMEM),) * 2,
        scratch_shapes=[
            pltpu.VMEM((n, feat), F32),
            pltpu.VMEM((n, feat), F32),
            pltpu.VMEM((1, HD), F32),
            pltpu.VMEM((1, HD), F32),
            pltpu.VMEM((tok // HD, HD), jnp.int32),
            pltpu.VMEM((n, tok, feat), BF16),
            pltpu.VMEM((n, tok, feat), BF16),
            pltpu.VMEM((2, ny, NX, feat, ff), BF16),
            pltpu.VMEM((ny, ff, NX * feat), BF16),
            pltpu.VMEM((ny, NX, feat, qkw), BF16),
            pltpu.VMEM((tok, ff), BF16),
            pltpu.VMEM((2, tok, ff), F32),
            pltpu.VMEM((tok, feat), F32),
            pltpu.VMEM((tok, qkw), F32),
            pltpu.VMEM((n, tok, feat), F32),
            pltpu.VMEM((2, most, CHUNKS, ch, feat), BF16),
            pltpu.VMEM((2, CHUNKS, ch, feat), BF16),
            pltpu.VMEM((tok, 2 * tok), BF16),
            pltpu.VMEM((2, tok, feat), BF16),
            pltpu.VMEM((2, tok, qkw), BF16),
            ring_sems, ring_sems, ring_sems, ring_sems, ring_sems, ring_sems,
            pltpu.SemaphoreType.DMA((6,)),
            pltpu.SemaphoreType.DMA((3,)),
            pltpu.SemaphoreType.DMA((3, 3)),
            pltpu.SemaphoreType.DMA((3, 3)),
            pltpu.SemaphoreType.DMA((3, 3)),
            pltpu.SemaphoreType.DMA((3, 3)),
            pltpu.SemaphoreType.DMA((3, 4)),
            pltpu.SemaphoreType.DMA((3, 4)),
            pltpu.SemaphoreType.DMA((2, CHUNKS)),
            pltpu.SemaphoreType.DMA((2, CHUNKS)),
        ],
        compiler_params=pltpu.CompilerParams(
            collective_id=0, has_side_effects=True, vmem_limit_bytes=60 * 1024 * 1024
        ),
        name="block_step",
    )(
        residual, post_gain.reshape(n, feat), w_gate, w_up, w_down, next_gain.reshape(n, feat), w_qkv,
        q_gain.reshape(1, -1), k_gain.reshape(1, -1), source.reshape(-1, HD),
    )


def solution(mesh):
    return jax.shard_map(
        per_device,
        mesh=mesh,
        in_specs=(
            P(("rep", "row"), "col"),
            P(),
            P("row", "col"),
            P("row", "col"),
            P("col", "row"),
            P(),
            P("row", "col"),
            P(),
            P(),
            P(("rep", "row")),
        ),
        out_specs=(P(("rep", "row"), "col"), P(("rep", "row"), "col")),
        check_vma=False,
    )
```
